512 devices in a mesh: row: 16 (over y, core), col: 32 (over z, x).
Axes of the slice: x: 4, y: 8, z: 8, core: 2. Of those that a mesh axis runs over, the one named last changes fastest.
Arguments:
- stream_speed: bfloat16 [512, 2048, 128], P('col', 'row'), may hold values from -6 to 6
- normal_speed: bfloat16 [512, 2048, 128], P('col', 'row'), may hold values from -6 to 6
- span_speed: bfloat16 [512, 2048, 128], P('col', 'row'), may hold values from -6 to 6
- stream_first: bfloat16 [2048, 2048], P('row'), may hold values from -0.125 to 0.125
- stream_second: bfloat16 [2048, 2048], P('row'), may hold values from -0.125 to 0.125
- wall_first: bfloat16 [512, 512], replicated, may hold values from -0.25 to 0.25
- wall_second: bfloat16 [512, 512], replicated, may hold values from -0.25 to 0.25
- metric1: float32 [512], replicated, may hold values from 0.5 to 2
- metric2: float32 [512], replicated, may hold values from -1.5 to 1.5
- span_coef: float32 [2, 9], replicated, may hold values from -1 to 1
- counts: int32 [32], replicated, may hold values from 1 to 4, as said below
Outputs:
- tendency: bfloat16 [512, 2048, 128], P('col', 'row')
The draws below stay inside these ranges and needn't reach their ends.
Inputs may be any that keep to these rules, and one draw needn't show every extreme that they name: counts[b] is the number of fluid planes at the start of spanwise block b of 4 planes; some block is all fluid.
All inputs are finite; a program needn't handle non-finite values.
Results may differ from the reference program's by a relative error of at most 0.0051.
Values may be sent and summed in bfloat16 or wider, within the bound.
A program may use at most 128 MiB of HBM per device.

```python
import math
import jax
import jax.numpy as jnp
from jax import lax

NX = 2048
NY = 512
ZB = 4
REACH = 4
NZ = 128


def draw_counts(key, part):
    block_total = NZ // ZB
    first_key, second_key = jax.random.split(jax.random.fold_in(key, 17))
    values = jax.random.randint(first_key, (block_total,), 1, ZB + 1)
    chosen = jax.random.randint(second_key, (), 0, block_total)
    return jnp.where(jnp.arange(block_total) == chosen, ZB, values).astype(jnp.int32)


def levels(rng, shape, shards, smallest, high):
    level, own = 1.0, jax.random.fold_in(rng, 6)
    for position, parts in shards:
        draws = jnp.exp(jax.random.uniform(jax.random.fold_in(own, position), (parts,), jnp.float32, smallest / len(shards), high / len(shards)))
        level = level * jnp.repeat(draws, shape[position] // parts).reshape([-1 if axis == position else 1 for axis in range(len(shape))])
    return level


def scatter_about(own_key, shape, width, most, shards=(), kind=jnp.bfloat16):
    values = jax.random.normal(own_key, shape, jnp.float32) * width
    if len(shards) > 0:
        values = levels(own_key, shape, shards, -0.22, 0.18) * values
    return jnp.clip(values, min=-most, max=most).astype(kind)


def setup_inputs(seed: int = 0) -> dict:
    streams_of = jax.random.split(jax.random.key(seed), 12)
    stream_speed = scatter_about(streams_of[0], (NY, NX, NZ), 1.0, 6.0, ((0, 32), (1, 16)))
    normal_speed = scatter_about(streams_of[1], (NY, NX, NZ), 1.0, 6.0, ((0, 32), (1, 16)))
    span_speed = scatter_about(streams_of[2], (NY, NX, NZ), 1.0, 6.0, ((0, 32), (1, 16)))
    stream_first = scatter_about(streams_of[3], (NX, NX), NX ** -0.5, 0.125, ((0, 16),))
    stream_second = scatter_about(streams_of[4], (NX, NX), NX ** -0.5, 0.125, ((0, 16),))
    wall_first = scatter_about(streams_of[5], (NY, NY), NY ** -0.5, 0.25)
    wall_second = scatter_about(streams_of[6], (NY, NY), NY ** -0.5, 0.25)
    metric1 = jnp.clip(jnp.exp(jax.random.uniform(streams_of[7], (NY,), jnp.float32, math.log(0.5), math.log(2.0))), 0.5, 2.0)
    metric2 = jnp.clip(jax.random.uniform(streams_of[8], (NY,), jnp.float32, -1.5, 1.5), -1.5, 1.5)
    span_coef = jnp.clip(jax.random.uniform(streams_of[9], (2, 2 * REACH + 1), jnp.float32, -1.0, 1.0), -1.0, 1.0)
    counts = draw_counts(jax.random.fold_in(streams_of[11], 71), 0)
    return dict(stream_speed=stream_speed, normal_speed=normal_speed, span_speed=span_speed, stream_first=stream_first, stream_second=stream_second, wall_first=wall_first, wall_second=wall_second, metric1=metric1, metric2=metric2, span_coef=span_coef, counts=counts)


viscosity = 0.25


def along_stream(matrix, field):
    flattened = jnp.transpose(field, (1, 0, 2)).reshape(NX, -1)
    outcome = jnp.dot(matrix, flattened, preferred_element_type=jnp.float32)
    return jnp.transpose(outcome.reshape(NX, NY, NZ), (1, 0, 2))


def reference(stream_speed, normal_speed, span_speed, stream_first, stream_second, wall_first, wall_second, metric1, metric2, span_coef, counts):
    stream_full = stream_speed.astype(jnp.float32)
    flux_stream = (stream_full * stream_full).astype(jnp.bfloat16)
    term_stream = viscosity * along_stream(stream_second, stream_speed) - along_stream(stream_first, flux_stream)
    flux_normal = (stream_full * normal_speed.astype(jnp.float32)).astype(jnp.bfloat16)
    flattened = stream_speed.reshape(NY, -1)
    first_stream = jnp.dot(wall_first, flattened, preferred_element_type=jnp.float32)
    second_stream = jnp.dot(wall_second, flattened, preferred_element_type=jnp.float32)
    first_flux = jnp.dot(wall_first, flux_normal.reshape(NY, -1), preferred_element_type=jnp.float32)
    weight_one = metric1[:, None]
    weight_two = metric2[:, None]
    term_wall = viscosity * (weight_one * weight_one * second_stream + weight_two * first_stream) - weight_one * first_flux
    term_wall = lax.optimization_barrier(term_wall.reshape(NY, NX, NZ).astype(jnp.bfloat16)).astype(jnp.float32)
    flux_span = lax.optimization_barrier((stream_full * span_speed.astype(jnp.float32)).astype(jnp.bfloat16)).astype(jnp.float32)
    radius = span_coef.shape[1] // 2
    term_span = jnp.zeros((NY, NX, NZ), jnp.float32)
    for offset_z in range(-radius, radius + 1):
        term_span = term_span + viscosity * span_coef[1, offset_z + radius] * jnp.roll(stream_full, -offset_z, 2)
        term_span = term_span - span_coef[0, offset_z + radius] * jnp.roll(flux_span, -offset_z, 2)
    plane_index = jnp.arange(NZ, dtype=jnp.int32)
    fluid_limit = counts[(plane_index // ZB).astype(jnp.int32)]
    fluid_mask = (plane_index % ZB < fluid_limit).astype(jnp.float32)
    return (fluid_mask * (term_stream + term_wall + term_span)).astype(jnp.bfloat16)
```

```python
import functools

import jax
import jax.numpy as jnp
from jax import lax
from jax.experimental import pallas as pl
from jax.experimental.pallas import tpu as pltpu
from jax.sharding import PartitionSpec as P

ZB = 4
VISCOSITY = 0.25
MESH = pl.DeviceIdType.MESH
F32 = jnp.float32
BF16 = jnp.bfloat16


def matmul(left, right):
    return jnp.dot(left, right, preferred_element_type=F32)


def swap_matrix(size):
    total = size * size
    row = lax.broadcasted_iota(jnp.int32, (total, total), 0)
    column = lax.broadcasted_iota(jnp.int32, (total, total), 1)
    same = (row // size == column % size) & (row % size == column // size)
    return jnp.where(same, 1.0, 0.0).astype(BF16)


def kernel(
    row_count,
    col_count,
    stream_hbm,
    normal_hbm,
    span_hbm,
    first_hbm,
    second_hbm,
    wall_first_hbm,
    wall_second_hbm,
    metric1_ref,
    metric2_ref,
    coef_ref,
    counts_ref,
    out_ref,
    gathered,
    normal,
    span,
    first,
    second,
    wall_first,
    wall_second,
    line_matrix,
    wall_matrix,
    lines_out,
    lines_in,
    terms_out,
    terms_in,
    total,
    swap,
    load_sem,
    ring_send,
    ring_recv,
    pair_send,
    pair_recv,
    lines_send,
    lines_recv,
    terms_send,
    terms_recv,
):
    chips = row_count // 2
    reach = chips // 2
    walls, length, planes = normal.shape
    half = walls // 2
    per_peer = length // col_count
    row = lax.axis_index("row")
    col = lax.axis_index("col")
    chip, core = row // 2, lax.rem(row, 2)
    right = lax.rem(row + 2, row_count)
    left = lax.rem(row + row_count - 2, row_count)
    sibling = row + 1 - 2 * core

    barrier = pltpu.get_barrier_semaphore()

    def greet(step, carry):
        peer = lax.rem(col + step, col_count)
        pl.semaphore_signal(barrier, inc=1, device_id=(row, peer), device_id_type=MESH)
        return carry

    for neighbour in (right, left, sibling):
        pl.semaphore_signal(barrier, inc=1, device_id=(neighbour, col), device_id_type=MESH)
    lax.fori_loop(1, col_count, greet, 0)

    pairs = (
        (stream_hbm, gathered.at[0, 0]),
        (normal_hbm, normal),
        (span_hbm, span),
        (second_hbm, second),
        (first_hbm, first),
        (wall_second_hbm, wall_second),
        (wall_first_hbm, wall_first),
    )
    loads = [pltpu.make_async_copy(a, b, load_sem.at[i]) for i, (a, b) in enumerate(pairs)]
    for load in loads:
        load.start()
    swap[...] = swap_matrix(walls)
    pl.semaphore_wait(barrier, col_count + 2)

    def up_slot(hop):
        return hop

    def down_slot(hop):
        return hop if hop == 0 or hop == reach else reach + hop

    def ring(way, part, hop):
        slot = up_slot if way == 0 else down_slot
        rows = pl.ds(part * half, half)
        source = stream_hbm.at[rows] if hop == 1 else gathered.at[0, slot(hop - 1), rows]
        return pltpu.make_async_remote_copy(
            src_ref=source,
            dst_ref=gathered.at[0, slot(hop), rows],
            send_sem=ring_send.at[way, part, hop - 1],
            recv_sem=ring_recv.at[way, part, hop - 1],
            device_id=(right if way == 0 else left, col),
            device_id_type=MESH,
        )

    def share(slot, part):
        rows = pl.ds(part * half, half)
        source = stream_hbm.at[rows] if slot == 0 else gathered.at[0, slot, rows]
        return pltpu.make_async_remote_copy(
            src_ref=source,
            dst_ref=gathered.at[1, slot, rows],
            send_sem=pair_send.at[slot, part],
            recv_sem=pair_recv.at[slot, part],
            device_id=(sibling, col),
            device_id_type=MESH,
        )

    def goes(way, part, hop):
        return hop <= (reach if way == part else reach - 1)

    order = ((0, 0), (1, 1), (0, 1), (1, 0))
    for way, part in order:
        if goes(way, part, 1):
            ring(way, part, 1).start()

    loads[0].wait()
    loads[1].wait()
    own = gathered.at[0, 0]
    for group in range(length // walls):
        rows = pl.ds(group * walls, walls)
        speed = own[:, rows, :]
        flux = speed * normal[:, rows, :]
        both = jnp.concatenate(
            [speed.reshape(walls * walls, planes), flux.reshape(walls * walls, planes)], axis=1
        )
        moved = matmul(swap[...], both).astype(BF16)
        for kind in range(2):
            piece = moved[:, kind * planes : (kind + 1) * planes]
            if per_peer <= walls:
                peers = walls // per_peer
                lines_out[pl.ds(group * peers, peers), kind] = piece.reshape(
                    peers, per_peer, walls, planes
                )
            else:
                peer, start = divmod(group * walls, per_peer)
                lines_out[peer, kind, pl.ds(start, walls)] = piece.reshape(walls, walls, planes)

    def send_lines(step, carry):
        peer = lax.rem(col + step, col_count)
        pltpu.make_async_remote_copy(
            src_ref=lines_out.at[peer],
            dst_ref=lines_in.at[col],
            send_sem=lines_send,
            recv_sem=lines_recv,
            device_id=(row, peer),
            device_id_type=MESH,
        ).start()
        return carry

    lax.fori_loop(1, col_count, send_lines, 0)
    pltpu.make_async_copy(lines_out.at[col], lines_in.at[col], lines_recv).start()
    for part in range(2):
        share(0, part).start()

    loads[2].wait()
    plane_in = lax.broadcasted_iota(jnp.int32, (planes, planes), 0)
    plane_out = lax.broadcasted_iota(jnp.int32, (planes, planes), 1)
    distance = lax.rem(plane_in - plane_out + planes, planes)
    radius = coef_ref.shape[1] // 2
    banded = []
    for kind, weight in ((1, VISCOSITY), (0, -1.0)):
        band = jnp.zeros((planes, planes), F32)
        for offset in range(-radius, radius + 1):
            value = weight * coef_ref[kind, offset + radius]
            band = jnp.where(distance == offset % planes, value, band)
        banded.append(band)
    band = jnp.concatenate(banded, axis=0)
    coarse = band.astype(BF16)
    fine = (band - coarse.astype(F32)).astype(BF16)
    band = jnp.concatenate([coarse, fine], axis=1)

    for wall in range(walls):
        speed = own[wall]
        both = jnp.concatenate([speed, speed * span[wall]], axis=1)
        result = matmul(both, band)
        total[wall] = result[:, :planes] + result[:, planes:]

    loads[3].wait()
    loads[4].wait()
    for block in range(row_count):
        columns = pl.ds(block * length, length)
        line_matrix[block, :, pl.ds(0, length)] = second[:, columns] * BF16(VISCOSITY)
        line_matrix[block, :, pl.ds(length, length)] = -first[:, columns]

    def accumulate(where, slot, part):
        if slot <= reach:
            owner = lax.rem(chip - slot + chips, chips)
        else:
            owner = lax.rem(chip + slot - reach, chips)
        owner = owner * 2 + (core if where == 0 else 1 - core)
        matrix = line_matrix[owner]
        block = gathered.at[where, slot]
        for pair in range(half // 2):
            wall = part * half + 2 * pair
            speed = jnp.concatenate([block[wall], block[wall + 1]], axis=1)
            result = matmul(matrix, jnp.concatenate([speed, speed * speed], axis=0))
            total[wall] += result[:, :planes]
            total[wall + 1] += result[:, planes:]

    def shared(slot, part):
        share(slot, part).wait_recv()
        accumulate(1, slot, part)

    for part in range(2):
        accumulate(0, 0, part)

    loads[5].wait()
    loads[6].wait()
    height = wall_first.shape[0]
    chunk = min(128, height)
    diagonal = lax.broadcasted_iota(jnp.int32, (chunk, chunk), 0) == lax.broadcasted_iota(
        jnp.int32, (chunk, chunk), 1
    )
    for start in range(0, height, chunk):
        rows = pl.ds(start, chunk)
        one = jnp.sum(jnp.where(diagonal, metric1_ref[:, rows], 0.0), axis=1, keepdims=True)
        two = jnp.sum(jnp.where(diagonal, metric2_ref[:, rows], 0.0), axis=1, keepdims=True)
        first_rows = wall_first[rows, :].astype(F32)
        second_rows = wall_second[rows, :].astype(F32)
        viscous = VISCOSITY * (one * one * second_rows + two * first_rows)
        wall_matrix[rows, pl.ds(0, height)] = viscous.astype(BF16)
        wall_matrix[rows, pl.ds(height, height)] = (-(one * first_rows)).astype(BF16)

    def wall_terms():
        pltpu.make_async_copy(lines_out, lines_in, lines_recv).wait()
        for position in range(0, per_peer, 2):
            kinds = []
            for kind in range(2):
                both = [
                    lines_in[:, kind, position + i].reshape(height, planes) for i in range(2)
                ]
                kinds.append(jnp.concatenate(both, axis=1))
            operand = jnp.concatenate(kinds, axis=0)
            result = matmul(wall_matrix[...], operand).astype(BF16)
            for i in range(2):
                terms_out[:, position + i] = result[:, i * planes : (i + 1) * planes].reshape(
                    col_count, walls, planes
                )

        def send_terms(step, carry):
            peer = lax.rem(col + step, col_count)
            pltpu.make_async_remote_copy(
                src_ref=terms_out.at[peer],
                dst_ref=terms_in.at[pl.ds(col * per_peer, per_peer)],
                send_sem=terms_send,
                recv_sem=terms_recv,
                device_id=(row, peer),
                device_id_type=MESH,
            ).start()
            return carry

        lax.fori_loop(1, col_count, send_terms, 0)
        pltpu.make_async_copy(
            terms_out.at[col], terms_in.at[pl.ds(col * per_peer, per_peer)], terms_recv
        ).start()

    pending = [(0, 0), (0, 1)]
    for hop in range(1, reach + 1):
        for stage in (order[:2], order[2:]):
            arrived = []
            for way, part in stage:
                if not goes(way, part, hop):
                    continue
                ring(way, part, hop).wait_recv()
                if goes(way, part, hop + 1):
                    ring(way, part, hop + 1).start()
                slot = (up_slot if way == 0 else down_slot)(hop)
                share(slot, part).start()
                arrived.append((slot, part))
            for slot, part in arrived:
                accumulate(0, slot, part)
            for slot, part in pending:
                shared(slot, part)
            pending = arrived
        if hop == max(reach // 2, 1):
            wall_terms()
    for slot, part in pending:
        shared(slot, part)

    position = lax.broadcasted_iota(jnp.int32, (1, planes), 1)
    limit = jnp.zeros((1, planes), jnp.int32)
    for block in range(counts_ref.shape[0]):
        limit = jnp.where(position // ZB == block, counts_ref[block], limit)
    mask = jnp.where(position % ZB < limit, 1.0, 0.0).astype(F32)

    pltpu.make_async_copy(
        terms_in, terms_in, terms_recv
    ).wait()
    for group in range(0, length // walls, 2):
        both = [
            terms_in[pl.ds((group + i) * walls, walls)].reshape(walls * walls, planes)
            for i in range(2)
        ]
        moved = matmul(swap[...], jnp.concatenate(both, axis=1))
        for i in range(2):
            rows = pl.ds((group + i) * walls, walls)
            term = moved[:, i * planes : (i + 1) * planes].reshape(walls, walls, planes)
            out_ref[:, rows, :] = (mask * (total[:, rows, :] + term)).astype(BF16)

    for hop in range(1, reach + 1):
        for way, part in order:
            if goes(way, part, hop):
                ring(way, part, hop).wait_send()
    for slot in range(chips):
        for part in range(2):
            share(slot, part).wait_send()
    others = pl.ds(0, col_count - 1)
    pltpu.make_async_copy(lines_out.at[others], lines_in.at[others], lines_send).wait()
    pltpu.make_async_copy(terms_out.at[others], terms_out.at[others], terms_send).wait()


def on_device(
    row_count,
    col_count,
    stream_speed,
    normal_speed,
    span_speed,
    stream_first,
    stream_second,
    wall_first,
    wall_second,
    metric1,
    metric2,
    span_coef,
    counts,
):
    shape = stream_speed.shape
    walls, length, planes = shape
    height = wall_first.shape[0]
    chips = row_count // 2
    reach = chips // 2
    per_peer = length // col_count
    anywhere = pl.BlockSpec(memory_space=pl.ANY)
    vector = pl.BlockSpec(memory_space=pltpu.VMEM)
    scalar = pl.BlockSpec(memory_space=pltpu.SMEM)
    exchange = (col_count, 2, per_peer, walls, planes)
    dma = pltpu.SemaphoreType.DMA
    return pl.pallas_call(
        functools.partial(kernel, row_count, col_count),
        out_shape=jax.ShapeDtypeStruct(shape, BF16),
        in_specs=[anywhere] * 7 + [vector] * 2 + [scalar] * 2,
        out_specs=vector,
        scratch_shapes=[
            pltpu.VMEM((2, chips, *shape), BF16),
            pltpu.VMEM(shape, BF16),
            pltpu.VMEM(shape, BF16),
            pltpu.VMEM(stream_first.shape, BF16),
            pltpu.VMEM(stream_second.shape, BF16),
            pltpu.VMEM(wall_first.shape, BF16),
            pltpu.VMEM(wall_second.shape, BF16),
            pltpu.VMEM((row_count, length, 2 * length), BF16),
            pltpu.VMEM((height, 2 * height), BF16),
            pltpu.VMEM(exchange, BF16),
            pltpu.VMEM(exchange, BF16),
            pltpu.VMEM((col_count, per_peer, walls, planes), BF16),
            pltpu.VMEM((length, walls, planes), BF16),
            pltpu.VMEM(shape, F32),
            pltpu.VMEM((walls * walls, walls * walls), BF16),
            dma((7,)),
            dma((2, 2, reach)),
            dma((2, 2, reach)),
            dma((chips, 2)),
            dma((chips, 2)),
            dma,
            dma,
            dma,
            dma,
        ],
        compiler_params=pltpu.CompilerParams(
            collective_id=0, has_side_effects=True, vmem_limit_bytes=48 * 2**20
        ),
    )(
        stream_speed,
        normal_speed,
        span_speed,
        stream_first,
        stream_second,
        wall_first,
        wall_second,
        metric1.reshape(1, -1),
        metric2.reshape(1, -1),
        span_coef,
        counts,
    )


def solution(mesh):
    placed = (
        P("col", "row", None),
        P("col", "row", None),
        P("col", "row", None),
        P("row", None),
        P("row", None),
        P(),
        P(),
        P(),
        P(),
        P(),
        P(),
    )
    return jax.shard_map(
        functools.partial(on_device, mesh.shape["row"], mesh.shape["col"]),
        mesh=mesh,
        in_specs=placed,
        out_specs=P("col", "row", None),
        check_vma=False,
    )
```

```python
import functools

import jax
import jax.numpy as jnp
from jax import lax
from jax.experimental import pallas as pl
from jax.experimental.pallas import tpu as pltpu
from jax.sharding import PartitionSpec as P

ZB = 4
VISCOSITY = 0.25
MESH = pl.DeviceIdType.MESH
F32 = jnp.float32
BF16 = jnp.bfloat16


def matmul(left, right):
    return jnp.dot(left, right, preferred_element_type=F32)


def swap_matrix(size):
    total = size * size
    row = lax.broadcasted_iota(jnp.int32, (total, total), 0)
    column = lax.broadcasted_iota(jnp.int32, (total, total), 1)
    same = (row // size == column % size) & (row % size == column // size)
    return jnp.where(same, 1.0, 0.0).astype(BF16)


def kernel(
    row_count,
    col_count,
    stream_hbm,
    normal_hbm,
    span_hbm,
    first_hbm,
    second_hbm,
    wall_first_hbm,
    wall_second_hbm,
    metric1_hbm,
    metric2_hbm,
    coef_hbm,
    counts_hbm,
    out_hbm,
    gathered,
    normal,
    span,
    first,
    second,
    wall_first,
    wall_second,
    line_matrix,
    wall_matrix,
    lines_out,
    lines_in,
    terms_out,
    terms_in,
    total,
    swap,
    out_ref,
    metric1_ref,
    metric2_ref,
    coef_ref,
    counts_ref,
    load_sem,
    ring_send,
    ring_recv,
    pair_send,
    pair_recv,
    lines_send,
    lines_recv,
    terms_send,
    terms_recv,
    early_ready,
    all_ready,
    store_sem,
):
    chips = row_count // 2
    reach = chips // 2
    walls, length, planes = normal.shape
    part_count = 4
    depth = walls // part_count
    per_peer = length // col_count
    row = lax.axis_index("row")
    col = lax.axis_index("col")
    chip, core = row // 2, lax.rem(row, 2)
    right = lax.rem(row + 2, row_count)
    left = lax.rem(row + row_count - 2, row_count)
    sibling = row + 1 - 2 * core

    middle = col_count // 2
    first_leader, last_leader = middle - 1, col_count - 1
    early, late = col < middle, col >= middle
    barrier = pltpu.get_barrier_semaphore()

    def signal(semaphore, place):
        pl.semaphore_signal(semaphore, inc=1, device_id=place, device_id_type=MESH)

    for neighbour in (right, left, sibling):
        signal(barrier, (neighbour, col))
    pl.when(early & (col != first_leader))(lambda: signal(barrier, (row, first_leader)))
    pl.when(late & (col != last_leader))(lambda: signal(barrier, (row, last_leader)))

    pairs = (
        (stream_hbm, gathered.at[0, 0]),
        (normal_hbm, normal),
        (span_hbm, span),
        (second_hbm, second),
        (first_hbm, first),
        (wall_second_hbm, wall_second),
        (wall_first_hbm, wall_first),
        (coef_hbm, coef_ref),
        (metric1_hbm, metric1_ref),
        (metric2_hbm, metric2_ref),
        (counts_hbm, counts_ref),
    )
    loads = [pltpu.make_async_copy(a, b, load_sem.at[i]) for i, (a, b) in enumerate(pairs)]
    for load in loads:
        load.start()
    swap[...] = swap_matrix(walls)

    @pl.when(early & (col != first_leader))
    def _():
        pl.semaphore_wait(barrier, 3)

    @pl.when(col == first_leader)
    def _():
        pl.semaphore_wait(barrier, 3 + middle - 1)

        def tell_late(peer, carry):
            signal(barrier, (row, peer))
            return carry

        def tell_early(peer, carry):
            signal(early_ready, (row, peer))
            return carry

        lax.fori_loop(middle, col_count, tell_late, 0)
        lax.fori_loop(0, middle - 1, tell_early, 0)

    @pl.when(late & (col != last_leader))
    def _():
        pl.semaphore_wait(barrier, 4)

    @pl.when(col == last_leader)
    def _():
        pl.semaphore_wait(barrier, 4 + col_count - middle - 1)

        def tell(peer, carry):
            signal(all_ready, (row, peer))
            return carry

        lax.fori_loop(0, col_count - 1, tell, 0)

    def up_slot(hop):
        return hop

    def down_slot(hop):
        return hop if hop == 0 or hop == reach else reach + hop

    def ring(way, part, hop):
        slot = up_slot if way == 0 else down_slot
        rows = pl.ds(part * depth, depth)
        source = stream_hbm.at[rows] if hop == 1 else gathered.at[0, slot(hop - 1), rows]
        return pltpu.make_async_remote_copy(
            src_ref=source,
            dst_ref=gathered.at[0, slot(hop), rows],
            send_sem=ring_send.at[way, part, hop - 1],
            recv_sem=ring_recv.at[way, part, hop - 1],
            device_id=(right if way == 0 else left, col),
            device_id_type=MESH,
        )

    def share(slot, part):
        rows = pl.ds(part * depth, depth)
        source = stream_hbm.at[rows] if slot == 0 else gathered.at[0, slot, rows]
        return pltpu.make_async_remote_copy(
            src_ref=source,
            dst_ref=gathered.at[1, slot, rows],
            send_sem=pair_send.at[slot, part],
            recv_sem=pair_recv.at[slot, part],
            device_id=(sibling, col),
            device_id_type=MESH,
        )

    def goes(way, part, hop):
        return hop <= (reach if way == part // (part_count // 2) else reach - 1)

    order = ((0, 0), (1, 2), (0, 1), (1, 3), (0, 2), (1, 0), (0, 3), (1, 1))
    for way, part in order:
        if goes(way, part, 1):
            ring(way, part, 1).start()

    loads[0].wait()
    loads[1].wait()
    own = gathered.at[0, 0]
    for group in range(length // walls):
        rows = pl.ds(group * walls, walls)
        speed = own[:, rows, :]
        flux = speed * normal[:, rows, :]
        both = jnp.concatenate(
            [speed.reshape(walls * walls, planes), flux.reshape(walls * walls, planes)], axis=1
        )
        moved = matmul(swap[...], both).astype(BF16)
        for kind in range(2):
            piece = moved[:, kind * planes : (kind + 1) * planes]
            if per_peer <= walls:
                peers = walls // per_peer
                lines_out[pl.ds(group * peers, peers), kind] = piece.reshape(
                    peers, per_peer, walls, planes
                )
            else:
                peer, start = divmod(group * walls, per_peer)
                lines_out[peer, kind, pl.ds(start, walls)] = piece.reshape(walls, walls, planes)

    def exchange(send_piece, start, stop):
        count = stop - start

        def body(step, carry):
            peer = start + lax.rem(col + step, count)
            pl.when(peer != col)(lambda: send_piece(peer))
            return carry

        lax.fori_loop(0, count, body, 0)

    def send_line(peer):
        pltpu.make_async_remote_copy(
            src_ref=lines_out.at[peer],
            dst_ref=lines_in.at[col],
            send_sem=lines_send,
            recv_sem=lines_recv,
            device_id=(row, peer),
            device_id_type=MESH,
        ).start()

    pltpu.make_async_copy(lines_out.at[col], lines_in.at[col], lines_recv).start()
    pl.when(late)(lambda: exchange(send_line, 0, middle))
    for part in range(part_count):
        share(0, part).start()

    loads[2].wait()
    loads[7].wait()
    plane_in = lax.broadcasted_iota(jnp.int32, (planes, planes), 0)
    plane_out = lax.broadcasted_iota(jnp.int32, (planes, planes), 1)
    distance = lax.rem(plane_in - plane_out + planes, planes)
    radius = coef_ref.shape[1] // 2
    banded = []
    for kind, weight in ((1, VISCOSITY), (0, -1.0)):
        band = jnp.zeros((planes, planes), F32)
        for offset in range(-radius, radius + 1):
            value = weight * coef_ref[kind, offset + radius]
            band = jnp.where(distance == offset % planes, value, band)
        banded.append(band)
    band = jnp.concatenate(banded, axis=0)
    coarse = band.astype(BF16)
    fine = (band - coarse.astype(F32)).astype(BF16)
    band = jnp.concatenate([coarse, fine], axis=1)

    for wall in range(walls):
        speed = own[wall]
        both = jnp.concatenate([speed, speed * span[wall]], axis=1)
        result = matmul(both, band)
        total[wall] = result[:, :planes] + result[:, planes:]

    @pl.when(late)
    def _():
        pl.when(col != last_leader)(lambda: pl.semaphore_wait(all_ready, 1))
        exchange(send_line, middle, col_count)

    loads[3].wait()
    loads[4].wait()
    for block in range(row_count):
        columns = pl.ds(block * length, length)
        line_matrix[block, :, pl.ds(0, length)] = second[:, columns] * BF16(VISCOSITY)
        line_matrix[block, :, pl.ds(length, length)] = -first[:, columns]

    def accumulate(where, slot, part):
        if slot <= reach:
            owner = lax.rem(chip - slot + chips, chips)
        else:
            owner = lax.rem(chip + slot - reach, chips)
        owner = owner * 2 + (core if where == 0 else 1 - core)
        matrix = line_matrix[owner]
        block = gathered.at[where, slot]
        for pair in range(depth // 2):
            wall = part * depth + 2 * pair
            speed = jnp.concatenate([block[wall], block[wall + 1]], axis=1)
            result = matmul(matrix, jnp.concatenate([speed, speed * speed], axis=0))
            total[wall] += result[:, :planes]
            total[wall + 1] += result[:, planes:]

    def shared(slot, part):
        share(slot, part).wait_recv()
        accumulate(1, slot, part)

    for part in range(part_count):
        accumulate(0, 0, part)

    for load in loads[5:7] + loads[8:10]:
        load.wait()
    height = wall_first.shape[0]
    chunk = min(128, height)
    diagonal = lax.broadcasted_iota(jnp.int32, (chunk, chunk), 0) == lax.broadcasted_iota(
        jnp.int32, (chunk, chunk), 1
    )
    for start in range(0, height, chunk):
        rows = pl.ds(start, chunk)
        one = jnp.sum(jnp.where(diagonal, metric1_ref[:, rows], 0.0), axis=1, keepdims=True)
        two = jnp.sum(jnp.where(diagonal, metric2_ref[:, rows], 0.0), axis=1, keepdims=True)
        first_rows = wall_first[rows, :].astype(F32)
        second_rows = wall_second[rows, :].astype(F32)
        viscous = VISCOSITY * (one * one * second_rows + two * first_rows)
        wall_matrix[rows, pl.ds(0, height)] = viscous.astype(BF16)
        wall_matrix[rows, pl.ds(height, height)] = (-(one * first_rows)).astype(BF16)

    def wall_terms():
        pltpu.make_async_copy(lines_out, lines_in, lines_recv).wait()
        for position in range(0, per_peer, 2):
            kinds = []
            for kind in range(2):
                both = [
                    lines_in[:, kind, position + i].reshape(height, planes) for i in range(2)
                ]
                kinds.append(jnp.concatenate(both, axis=1))
            operand = jnp.concatenate(kinds, axis=0)
            result = matmul(wall_matrix[...], operand).astype(BF16)
            for i in range(2):
                terms_out[:, position + i] = result[:, i * planes : (i + 1) * planes].reshape(
                    col_count, walls, planes
                )

        def send_term(peer):
            pltpu.make_async_remote_copy(
                src_ref=terms_out.at[peer],
                dst_ref=terms_in.at[pl.ds(col * per_peer, per_peer)],
                send_sem=terms_send,
                recv_sem=terms_recv,
                device_id=(row, peer),
                device_id_type=MESH,
            ).start()

        exchange(send_term, 0, col_count)
        pltpu.make_async_copy(
            terms_out.at[col], terms_in.at[pl.ds(col * per_peer, per_peer)], terms_recv
        ).start()

    @pl.when(early)
    def _():
        pl.when(col != first_leader)(lambda: pl.semaphore_wait(early_ready, 1))
        exchange(send_line, 0, middle)

    pending = [(0, part) for part in range(part_count)]
    for hop in range(1, reach + 1):
        for half in range(2):
            arrived = []
            for way, part in order[half * part_count : (half + 1) * part_count]:
                if not goes(way, part, hop):
                    continue
                ring(way, part, hop).wait_recv()
                if goes(way, part, hop + 1):
                    ring(way, part, hop + 1).start()
                slot = (up_slot if way == 0 else down_slot)(hop)
                share(slot, part).start()
                arrived.append((slot, part))
            for slot, part in arrived:
                accumulate(0, slot, part)
            for slot, part in pending:
                shared(slot, part)
            pending = arrived
            if (hop, half) == (1, 0):

                @pl.when(early)
                def _():
                    pl.semaphore_wait(all_ready, 1)
                    exchange(send_line, middle, col_count)

            if (hop, half) == (max(reach // 2, 1), 1):
                pl.when(late)(wall_terms)
            if (hop, half) == (max(reach // 2 + 1, 1), 0):
                pl.when(early)(wall_terms)
    for slot, part in pending:
        shared(slot, part)

    loads[10].wait()
    position = lax.broadcasted_iota(jnp.int32, (1, planes), 1)
    limit = jnp.zeros((1, planes), jnp.int32)
    for block in range(counts_ref.shape[0]):
        limit = jnp.where(position // ZB == block, counts_ref[block], limit)
    mask = jnp.where(position % ZB < limit, 1.0, 0.0).astype(F32)

    pltpu.make_async_copy(
        terms_in, terms_in, terms_recv
    ).wait()
    stores = []
    for group in range(0, length // walls, 2):
        both = [
            terms_in[pl.ds((group + i) * walls, walls)].reshape(walls * walls, planes)
            for i in range(2)
        ]
        moved = matmul(swap[...], jnp.concatenate(both, axis=1))
        for i in range(2):
            rows = pl.ds((group + i) * walls, walls)
            term = moved[:, i * planes : (i + 1) * planes].reshape(walls, walls, planes)
            out_ref[:, rows, :] = (mask * (total[:, rows, :] + term)).astype(BF16)
        rows = pl.ds(group * walls, 2 * walls)
        store = pltpu.make_async_copy(
            out_ref.at[:, rows], out_hbm.at[:, rows], store_sem.at[group // 2]
        )
        store.start()
        stores.append(store)

    for hop in range(1, reach + 1):
        for way, part in order:
            if goes(way, part, hop):
                ring(way, part, hop).wait_send()
    for slot in range(chips):
        for part in range(part_count):
            share(slot, part).wait_send()
    others = pl.ds(0, col_count - 1)
    pltpu.make_async_copy(lines_out.at[others], lines_in.at[others], lines_send).wait()
    pltpu.make_async_copy(terms_out.at[others], terms_out.at[others], terms_send).wait()
    for store in stores:
        store.wait()


def on_device(
    row_count,
    col_count,
    stream_speed,
    normal_speed,
    span_speed,
    stream_first,
    stream_second,
    wall_first,
    wall_second,
    metric1,
    metric2,
    span_coef,
    counts,
):
    shape = stream_speed.shape
    walls, length, planes = shape
    height = wall_first.shape[0]
    chips = row_count // 2
    reach = chips // 2
    per_peer = length // col_count
    hbm = pl.BlockSpec(memory_space=pltpu.HBM)
    exchange = (col_count, 2, per_peer, walls, planes)
    dma = pltpu.SemaphoreType.DMA
    return pl.pallas_call(
        functools.partial(kernel, row_count, col_count),
        out_shape=jax.ShapeDtypeStruct(shape, BF16),
        in_specs=[hbm] * 11,
        out_specs=hbm,
        scratch_shapes=[
            pltpu.VMEM((2, chips, *shape), BF16),
            pltpu.VMEM(shape, BF16),
            pltpu.VMEM(shape, BF16),
            pltpu.VMEM(stream_first.shape, BF16),
            pltpu.VMEM(stream_second.shape, BF16),
            pltpu.VMEM(wall_first.shape, BF16),
            pltpu.VMEM(wall_second.shape, BF16),
            pltpu.VMEM((row_count, length, 2 * length), BF16),
            pltpu.VMEM((height, 2 * height), BF16),
            pltpu.VMEM(exchange, BF16),
            pltpu.VMEM(exchange, BF16),
            pltpu.VMEM((col_count, per_peer, walls, planes), BF16),
            pltpu.VMEM((length, walls, planes), BF16),
            pltpu.VMEM(shape, F32),
            pltpu.VMEM((walls * walls, walls * walls), BF16),
            pltpu.VMEM(shape, BF16),
            pltpu.VMEM((1, height), F32),
            pltpu.VMEM((1, height), F32),
            pltpu.SMEM(span_coef.shape, F32),
            pltpu.SMEM(counts.shape, jnp.int32),
            dma((11,)),
            dma((2, 4, reach)),
            dma((2, 4, reach)),
            dma((chips, 4)),
            dma((chips, 4)),
            dma,
            dma,
            dma,
            dma,
            pltpu.SemaphoreType.REGULAR,
            pltpu.SemaphoreType.REGULAR,
            dma((length // walls // 2,)),
        ],
        compiler_params=pltpu.CompilerParams(
            collective_id=0, has_side_effects=True, vmem_limit_bytes=60 * 2**20
        ),
    )(
        stream_speed,
        normal_speed,
        span_speed,
        stream_first,
        stream_second,
        wall_first,
        wall_second,
        metric1.reshape(1, -1),
        metric2.reshape(1, -1),
        span_coef,
        counts,
    )


def solution(mesh):
    placed = (
        P("col", "row", None),
        P("col", "row", None),
        P("col", "row", None),
        P("row", None),
        P("row", None),
        P(),
        P(),
        P(),
        P(),
        P(),
        P(),
    )
    return jax.shard_map(
        functools.partial(on_device, mesh.shape["row"], mesh.shape["col"]),
        mesh=mesh,
        in_specs=placed,
        out_specs=P("col", "row", None),
        check_vma=False,
    )
```

```python
import functools

import jax
import jax.numpy as jnp
from jax import lax
from jax.experimental import pallas as pl
from jax.experimental.pallas import tpu as pltpu
from jax.sharding import PartitionSpec as P

ZB = 4
TORUS_WIDTH = 4
VISCOSITY = 0.25
MESH = pl.DeviceIdType.MESH
F32 = jnp.float32
BF16 = jnp.bfloat16


def matmul(left, right):
    return jnp.dot(left, right, preferred_element_type=F32)


def swap_matrix(size):
    total = size * size
    row = lax.broadcasted_iota(jnp.int32, (total, total), 0)
    column = lax.broadcasted_iota(jnp.int32, (total, total), 1)
    same = (row // size == column % size) & (row % size == column // size)
    return jnp.where(same, 1.0, 0.0).astype(BF16)


def kernel(
    row_count,
    col_count,
    stream_hbm,
    normal_hbm,
    span_hbm,
    first_hbm,
    second_hbm,
    wall_first_hbm,
    wall_second_hbm,
    metric1_hbm,
    metric2_hbm,
    coef_hbm,
    counts_hbm,
    out_hbm,
    gathered,
    normal,
    span,
    first,
    second,
    wall_first,
    wall_second,
    line_matrix,
    wall_matrix,
    lines_out,
    lines_in,
    terms_out,
    terms_in,
    total,
    swap,
    out_ref,
    metric1_ref,
    metric2_ref,
    coef_ref,
    counts_ref,
    load_sem,
    ring_send,
    ring_recv,
    pair_send,
    pair_recv,
    lines_send,
    lines_recv,
    terms_send,
    terms_recv,
    early_ready,
    all_ready,
    late_ready,
    store_sem,
):
    chips = row_count // 2
    reach = chips // 2
    walls, length, planes = normal.shape
    part_count = 4
    depth = walls // part_count
    per_peer = length // col_count
    row = lax.axis_index("row")
    col = lax.axis_index("col")
    chip, core = row // 2, lax.rem(row, 2)
    right = lax.rem(row + 2, row_count)
    left = lax.rem(row + row_count - 2, row_count)
    sibling = row + 1 - 2 * core

    pairs = (
        (stream_hbm, gathered.at[0, 0]),
        (normal_hbm, normal),
        (span_hbm, span),
        (second_hbm, second),
        (first_hbm, first),
        (wall_second_hbm, wall_second),
        (wall_first_hbm, wall_first),
        (coef_hbm, coef_ref),
        (metric1_hbm, metric1_ref),
        (metric2_hbm, metric2_ref),
        (counts_hbm, counts_ref),
    )
    loads = [pltpu.make_async_copy(a, b, load_sem.at[i]) for i, (a, b) in enumerate(pairs)]
    for load in loads:
        load.start()

    middle = col_count // 2
    first_leader, last_leader = middle - 1, col_count - 1
    early, late = col < middle, col >= middle
    width = min(TORUS_WIDTH, middle)
    rounds = col_count // width
    across, along = lax.rem(col, width), col // width
    far = [0] + [w for d in range(1, rounds // 2 + 1) for w in dict.fromkeys((d, rounds - d))]
    offsets = [(ahead, beside) for beside in range(width) for ahead in far if ahead or beside]
    barrier = pltpu.get_barrier_semaphore()

    def signal(semaphore, place):
        pl.semaphore_signal(semaphore, inc=1, device_id=place, device_id_type=MESH)

    for neighbour in (right, left, sibling):
        signal(barrier, (neighbour, col))
    pl.when(early & (col != first_leader))(lambda: signal(barrier, (row, first_leader)))
    pl.when(late & (col != last_leader))(lambda: signal(barrier, (row, last_leader)))

    swap[...] = swap_matrix(walls)

    @pl.when(early & (col != first_leader))
    def _():
        pl.semaphore_wait(barrier, 3)

    @pl.when(col == first_leader)
    def _():
        pl.semaphore_wait(barrier, 3 + middle - 1)

        def tell_late(peer, carry):
            signal(barrier, (row, peer))
            return carry

        def tell_early(peer, carry):
            signal(early_ready, (row, peer))
            return carry

        lax.fori_loop(middle, col_count, tell_late, 0)
        lax.fori_loop(0, middle - 1, tell_early, 0)

    @pl.when(late & (col != last_leader))
    def _():
        pl.semaphore_wait(barrier, 4)

    @pl.when(col == last_leader)
    def _():
        pl.semaphore_wait(barrier, 4 + col_count - middle - 1)

        def tell(peer, carry):
            signal(all_ready, (row, peer))
            return carry

        lax.fori_loop(middle, col_count - 1, tell, 0)

    @pl.when(late)
    def _():
        def tell(peer, carry):
            signal(late_ready.at[along - rounds // 2], (row, peer))
            return carry

        lax.fori_loop(0, middle, tell, 0)

    def up_slot(hop):
        return hop

    def down_slot(hop):
        return hop if hop == 0 or hop == reach else reach + hop

    def ring(way, part, hop):
        slot = up_slot if way == 0 else down_slot
        rows = pl.ds(part * depth, depth)
        source = stream_hbm.at[rows] if hop == 1 else gathered.at[0, slot(hop - 1), rows]
        return pltpu.make_async_remote_copy(
            src_ref=source,
            dst_ref=gathered.at[0, slot(hop), rows],
            send_sem=ring_send.at[way, part, hop - 1],
            recv_sem=ring_recv.at[way, part, hop - 1],
            device_id=(right if way == 0 else left, col),
            device_id_type=MESH,
        )

    def share(slot, part):
        rows = pl.ds(part * depth, depth)
        source = stream_hbm.at[rows] if slot == 0 else gathered.at[0, slot, rows]
        return pltpu.make_async_remote_copy(
            src_ref=source,
            dst_ref=gathered.at[1, slot, rows],
            send_sem=pair_send.at[slot, part],
            recv_sem=pair_recv.at[slot, part],
            device_id=(sibling, col),
            device_id_type=MESH,
        )

    def goes(way, part, hop):
        return hop <= (reach if way == part // (part_count // 2) else reach - 1)

    order = ((0, 0), (1, 2), (0, 1), (1, 3), (0, 2), (1, 0), (0, 3), (1, 1))
    for way, part in order:
        if goes(way, part, 1):
            ring(way, part, 1).start()
    for part in range(part_count):
        share(0, part).start()

    def exchange(send_piece, wanted=None):
        for ahead, beside in offsets:
            peer = lax.rem(along + ahead, rounds) * width + lax.rem(across + beside, width)
            if wanted is None:
                send_piece(peer)
            else:
                pl.when(wanted(peer))(functools.partial(send_piece, peer))

    def is_early(peer):
        return peer < middle

    def is_late(peer):
        return peer >= middle

    def send_line(chunk, peer):
        pltpu.make_async_remote_copy(
            src_ref=lines_out.at[chunk, peer],
            dst_ref=lines_in.at[chunk, col],
            send_sem=lines_send,
            recv_sem=lines_recv.at[chunk],
            device_id=(row, peer),
            device_id_type=MESH,
        ).start()

    first_lines = functools.partial(send_line, 0)
    second_lines = functools.partial(send_line, 1)

    loads[0].wait()
    loads[1].wait()
    own = gathered.at[0, 0]
    chunk_size = per_peer // 2

    def make_lines(group):
        rows = pl.ds(group * walls, walls)
        speed = own[:, rows, :]
        flux = speed * normal[:, rows, :]
        both = jnp.concatenate(
            [speed.reshape(walls * walls, planes), flux.reshape(walls * walls, planes)], axis=1
        )
        moved = matmul(swap[...], both).astype(BF16)
        for kind in range(2):
            piece = moved[:, kind * planes : (kind + 1) * planes]
            if per_peer <= walls:
                peers = walls // per_peer
                piece = piece.reshape(peers, 2, chunk_size, walls, planes)
                for chunk in range(2):
                    lines_out[chunk, pl.ds(group * peers, peers), kind] = piece[:, chunk]
            else:
                peer, rest = divmod(group * walls, per_peer)
                chunk, start = divmod(rest, chunk_size)
                piece = piece.reshape(walls, walls, planes)
                lines_out[chunk, peer, kind, pl.ds(start, walls)] = piece

    groups = length // walls
    for group in range(groups // 2):
        make_lines(group)
    pl.when(late)(lambda: exchange(first_lines, is_early))
    for group in range(groups // 2, groups):
        make_lines(group)
    for chunk in range(2):
        pltpu.make_async_copy(
            lines_out.at[chunk, col], lines_in.at[chunk, col], lines_recv.at[chunk]
        ).start()

    @pl.when(late)
    def _():
        pl.when(col != last_leader)(lambda: pl.semaphore_wait(all_ready, 1))
        exchange(first_lines, is_late)
        exchange(second_lines)

    loads[2].wait()
    loads[7].wait()
    plane_in = lax.broadcasted_iota(jnp.int32, (planes, planes), 0)
    plane_out = lax.broadcasted_iota(jnp.int32, (planes, planes), 1)
    distance = lax.rem(plane_in - plane_out + planes, planes)
    radius = coef_ref.shape[1] // 2
    banded = []
    for kind, weight in ((1, VISCOSITY), (0, -1.0)):
        band = jnp.zeros((planes, planes), F32)
        for offset in range(-radius, radius + 1):
            value = weight * coef_ref[kind, offset + radius]
            band = jnp.where(distance == offset % planes, value, band)
        banded.append(band)
    band = jnp.concatenate(banded, axis=0)
    coarse = band.astype(BF16)
    fine = (band - coarse.astype(F32)).astype(BF16)
    band = jnp.concatenate([coarse, fine], axis=1)

    for wall in range(walls):
        speed = own[wall]
        both = jnp.concatenate([speed, speed * span[wall]], axis=1)
        result = matmul(both, band)
        total[wall] = result[:, :planes] + result[:, planes:]

    loads[3].wait()
    loads[4].wait()
    for block in range(row_count):
        columns = pl.ds(block * length, length)
        line_matrix[block, :, pl.ds(0, length)] = second[:, columns] * BF16(VISCOSITY)
        line_matrix[block, :, pl.ds(length, length)] = -first[:, columns]

    def accumulate(where, slot, part):
        if slot <= reach:
            owner = lax.rem(chip - slot + chips, chips)
        else:
            owner = lax.rem(chip + slot - reach, chips)
        owner = owner * 2 + (core if where == 0 else 1 - core)
        matrix = line_matrix[owner]
        block = gathered.at[where, slot]
        for pair in range(depth // 2):
            wall = part * depth + 2 * pair
            speed = jnp.concatenate([block[wall], block[wall + 1]], axis=1)
            result = matmul(matrix, jnp.concatenate([speed, speed * speed], axis=0))
            total[wall] += result[:, :planes]
            total[wall + 1] += result[:, planes:]

    def shared(slot, part):
        share(slot, part).wait_recv()
        accumulate(1, slot, part)

    for part in range(part_count):
        accumulate(0, 0, part)

    for load in loads[5:7] + loads[8:10]:
        load.wait()
    height = wall_first.shape[0]
    chunk = min(128, height)
    diagonal = lax.broadcasted_iota(jnp.int32, (chunk, chunk), 0) == lax.broadcasted_iota(
        jnp.int32, (chunk, chunk), 1
    )
    for start in range(0, height, chunk):
        rows = pl.ds(start, chunk)
        one = jnp.sum(jnp.where(diagonal, metric1_ref[:, rows], 0.0), axis=1, keepdims=True)
        two = jnp.sum(jnp.where(diagonal, metric2_ref[:, rows], 0.0), axis=1, keepdims=True)
        first_rows = wall_first[rows, :].astype(F32)
        second_rows = wall_second[rows, :].astype(F32)
        viscous = VISCOSITY * (one * one * second_rows + two * first_rows)
        wall_matrix[rows, pl.ds(0, height)] = viscous.astype(BF16)
        wall_matrix[rows, pl.ds(height, height)] = (-(one * first_rows)).astype(BF16)

    def wall_terms(chunk):
        pltpu.make_async_copy(lines_out.at[chunk], lines_in.at[chunk], lines_recv.at[chunk]).wait()
        for position in range(0, chunk_size, 2):
            kinds = []
            for kind in range(2):
                both = [
                    lines_in[chunk, :, kind, position + i].reshape(height, planes)
                    for i in range(2)
                ]
                kinds.append(jnp.concatenate(both, axis=1))
            operand = jnp.concatenate(kinds, axis=0)
            result = matmul(wall_matrix[...], operand).astype(BF16)
            for i in range(2):
                terms_out[chunk, :, position + i] = result[
                    :, i * planes : (i + 1) * planes
                ].reshape(col_count, walls, planes)

        place = terms_in.at[pl.ds(col * per_peer + chunk * chunk_size, chunk_size)]

        def send_term(peer):
            pltpu.make_async_remote_copy(
                src_ref=terms_out.at[chunk, peer],
                dst_ref=place,
                send_sem=terms_send,
                recv_sem=terms_recv,
                device_id=(row, peer),
                device_id_type=MESH,
            ).start()

        exchange(send_term)
        pltpu.make_async_copy(terms_out.at[chunk, col], place, terms_recv).start()

    first_quarter = col < middle // 2
    second_quarter = early & (col >= middle // 2)

    @pl.when(early)
    def _():
        pl.when(col != first_leader)(lambda: pl.semaphore_wait(early_ready, 1))
        exchange(first_lines, is_early)

    def lines_to_late():
        for plane in range(rounds // 2):
            pl.semaphore_wait(late_ready.at[plane], width)
            for beside in range(width):
                first_lines(middle + plane * width + lax.rem(across + beside, width))
        exchange(second_lines)

    pl.when(second_quarter)(lines_to_late)
    slots = {
        (1, 0): [(first_quarter, lines_to_late)],
        (1, 1): [(late, functools.partial(wall_terms, 0))],
        (2, 0): [(second_quarter, functools.partial(wall_terms, 0))],
        (2, 1): [
            (first_quarter, functools.partial(wall_terms, 0)),
            (late, functools.partial(wall_terms, 1)),
        ],
        (3, 0): [(second_quarter, functools.partial(wall_terms, 1))],
        (3, 1): [(first_quarter, functools.partial(wall_terms, 1))],
    }

    pending = [(0, part) for part in range(part_count)]
    for hop in range(1, reach + 1):
        for half in range(2):
            arrived = []
            for way, part in order[half * part_count : (half + 1) * part_count]:
                if not goes(way, part, hop):
                    continue
                ring(way, part, hop).wait_recv()
                if goes(way, part, hop + 1):
                    ring(way, part, hop + 1).start()
                slot = (up_slot if way == 0 else down_slot)(hop)
                share(slot, part).start()
                arrived.append((slot, part))
            for slot, part in arrived:
                accumulate(0, slot, part)
            for slot, part in pending:
                shared(slot, part)
            pending = arrived
            for (at_hop, at_half), actions in slots.items():
                if (min(at_hop, reach), at_half) == (hop, half):
                    for condition, action in actions:
                        pl.when(condition)(action)
    for slot, part in pending:
        shared(slot, part)

    loads[10].wait()
    position = lax.broadcasted_iota(jnp.int32, (1, planes), 1)
    limit = jnp.zeros((1, planes), jnp.int32)
    for block in range(counts_ref.shape[0]):
        limit = jnp.where(position // ZB == block, counts_ref[block], limit)
    mask = jnp.where(position % ZB < limit, 1.0, 0.0).astype(F32)

    pltpu.make_async_copy(
        terms_in, terms_in, terms_recv
    ).wait()
    stores = []
    for group in range(0, length // walls, 2):
        both = [
            terms_in[pl.ds((group + i) * walls, walls)].reshape(walls * walls, planes)
            for i in range(2)
        ]
        moved = matmul(swap[...], jnp.concatenate(both, axis=1))
        for i in range(2):
            rows = pl.ds((group + i) * walls, walls)
            term = moved[:, i * planes : (i + 1) * planes].reshape(walls, walls, planes)
            out_ref[:, rows, :] = (mask * (total[:, rows, :] + term)).astype(BF16)
        rows = pl.ds(group * walls, 2 * walls)
        store = pltpu.make_async_copy(
            out_ref.at[:, rows], out_hbm.at[:, rows], store_sem.at[group // 2]
        )
        store.start()
        stores.append(store)

    for hop in range(1, reach + 1):
        for way, part in order:
            if goes(way, part, hop):
                ring(way, part, hop).wait_send()
    for slot in range(chips):
        for part in range(part_count):
            share(slot, part).wait_send()
    others = pl.ds(0, col_count - 1)
    pltpu.make_async_copy(lines_out.at[:, others], lines_in.at[:, others], lines_send).wait()
    pltpu.make_async_copy(terms_out.at[:, others], terms_out.at[:, others], terms_send).wait()
    for store in stores:
        store.wait()


def on_device(
    row_count,
    col_count,
    stream_speed,
    normal_speed,
    span_speed,
    stream_first,
    stream_second,
    wall_first,
    wall_second,
    metric1,
    metric2,
    span_coef,
    counts,
):
    shape = stream_speed.shape
    walls, length, planes = shape
    height = wall_first.shape[0]
    chips = row_count // 2
    reach = chips // 2
    per_peer = length // col_count
    hbm = pl.BlockSpec(memory_space=pltpu.HBM)
    exchange = (2, col_count, 2, per_peer // 2, walls, planes)
    dma = pltpu.SemaphoreType.DMA
    return pl.pallas_call(
        functools.partial(kernel, row_count, col_count),
        out_shape=jax.ShapeDtypeStruct(shape, BF16),
        in_specs=[hbm] * 11,
        out_specs=hbm,
        scratch_shapes=[
            pltpu.VMEM((2, chips, *shape), BF16),
            pltpu.VMEM(shape, BF16),
            pltpu.VMEM(shape, BF16),
            pltpu.VMEM(stream_first.shape, BF16),
            pltpu.VMEM(stream_second.shape, BF16),
            pltpu.VMEM(wall_first.shape, BF16),
            pltpu.VMEM(wall_second.shape, BF16),
            pltpu.VMEM((row_count, length, 2 * length), BF16),
            pltpu.VMEM((height, 2 * height), BF16),
            pltpu.VMEM(exchange, BF16),
            pltpu.VMEM(exchange, BF16),
            pltpu.VMEM((2, col_count, per_peer // 2, walls, planes), BF16),
            pltpu.VMEM((length, walls, planes), BF16),
            pltpu.VMEM(shape, F32),
            pltpu.VMEM((walls * walls, walls * walls), BF16),
            pltpu.VMEM(shape, BF16),
            pltpu.VMEM((1, height), F32),
            pltpu.VMEM((1, height), F32),
            pltpu.SMEM(span_coef.shape, F32),
            pltpu.SMEM(counts.shape, jnp.int32),
            dma((11,)),
            dma((2, 4, reach)),
            dma((2, 4, reach)),
            dma((chips, 4)),
            dma((chips, 4)),
            dma,
            dma((2,)),
            dma,
            dma,
            pltpu.SemaphoreType.REGULAR,
            pltpu.SemaphoreType.REGULAR,
            pltpu.SemaphoreType.REGULAR((max(col_count // TORUS_WIDTH, 2) // 2,)),
            dma((length // walls // 2,)),
        ],
        compiler_params=pltpu.CompilerParams(
            collective_id=0, has_side_effects=True, vmem_limit_bytes=60 * 2**20
        ),
    )(
        stream_speed,
        normal_speed,
        span_speed,
        stream_first,
        stream_second,
        wall_first,
        wall_second,
        metric1.reshape(1, -1),
        metric2.reshape(1, -1),
        span_coef,
        counts,
    )


def solution(mesh):
    placed = (
        P("col", "row", None),
        P("col", "row", None),
        P("col", "row", None),
        P("row", None),
        P("row", None),
        P(),
        P(),
        P(),
        P(),
        P(),
        P(),
    )
    return jax.shard_map(
        functools.partial(on_device, mesh.shape["row"], mesh.shape["col"]),
        mesh=mesh,
        in_specs=placed,
        out_specs=P("col", "row", None),
        check_vma=False,
    )
```

```python
import functools

import jax
import jax.numpy as jnp
from jax import lax
from jax.experimental import pallas as pl
from jax.experimental.pallas import tpu as pltpu
from jax.sharding import PartitionSpec as P

ZB = 4
TORUS_WIDTH = 4
VISCOSITY = 0.25
MESH = pl.DeviceIdType.MESH
F32 = jnp.float32
BF16 = jnp.bfloat16


def matmul(left, right):
    return jnp.dot(left, right, preferred_element_type=F32)


def swap_matrix(size):
    total = size * size
    row = lax.broadcasted_iota(jnp.int32, (total, total), 0)
    column = lax.broadcasted_iota(jnp.int32, (total, total), 1)
    same = (row // size == column % size) & (row % size == column // size)
    return jnp.where(same, 1.0, 0.0).astype(BF16)


def kernel(
    row_count,
    col_count,
    stream_hbm,
    normal_hbm,
    span_hbm,
    first_hbm,
    second_hbm,
    wall_first_hbm,
    wall_second_hbm,
    metric1_hbm,
    metric2_hbm,
    coef_hbm,
    counts_hbm,
    out_ref,
    gathered,
    normal,
    span,
    first,
    second,
    wall_first,
    wall_second,
    line_matrix,
    wall_matrix,
    lines_out,
    lines_in,
    terms_out,
    terms_in,
    total,
    swap,
    metric1_ref,
    metric2_ref,
    coef_ref,
    counts_ref,
    load_sem,
    ring_send,
    ring_recv,
    pair_send,
    pair_recv,
    lines_send,
    lines_recv,
    terms_send,
    terms_recv,
    early_ready,
    all_ready,
    late_ready,
):
    chips = row_count // 2
    reach = chips // 2
    walls, length, planes = normal.shape
    part_count = 4
    depth = walls // part_count
    per_peer = length // col_count
    row = lax.axis_index("row")
    col = lax.axis_index("col")
    chip, core = row // 2, lax.rem(row, 2)
    right = lax.rem(row + 2, row_count)
    left = lax.rem(row + row_count - 2, row_count)
    sibling = row + 1 - 2 * core

    pairs = (
        (stream_hbm, gathered.at[0, 0]),
        (normal_hbm, normal),
        (span_hbm, span),
        (second_hbm, second),
        (first_hbm, first),
        (wall_second_hbm, wall_second),
        (wall_first_hbm, wall_first),
        (coef_hbm, coef_ref),
        (metric1_hbm, metric1_ref),
        (metric2_hbm, metric2_ref),
        (counts_hbm, counts_ref),
    )
    loads = [pltpu.make_async_copy(a, b, load_sem.at[i]) for i, (a, b) in enumerate(pairs)]
    for load in loads:
        load.start()

    middle = col_count // 2
    first_leader, last_leader = middle - 1, col_count - 1
    early, late = col < middle, col >= middle
    width = min(TORUS_WIDTH, middle)
    rounds = col_count // width
    across, along = lax.rem(col, width), col // width
    far = [0] + [w for d in range(1, rounds // 2 + 1) for w in dict.fromkeys((d, rounds - d))]
    offsets = [(ahead, beside) for beside in range(width) for ahead in far if ahead or beside]
    barrier = pltpu.get_barrier_semaphore()

    def signal(semaphore, place):
        pl.semaphore_signal(semaphore, inc=1, device_id=place, device_id_type=MESH)

    for neighbour in (right, left, sibling):
        signal(barrier, (neighbour, col))
    pl.when(early & (col != first_leader))(lambda: signal(barrier, (row, first_leader)))
    pl.when(late & (col != last_leader))(lambda: signal(barrier, (row, last_leader)))

    swap[...] = swap_matrix(walls)

    @pl.when(early & (col != first_leader))
    def _():
        pl.semaphore_wait(barrier, 3)

    @pl.when(col == first_leader)
    def _():
        pl.semaphore_wait(barrier, 3 + middle - 1)

        def tell_late(peer, carry):
            signal(barrier, (row, peer))
            return carry

        def tell_early(peer, carry):
            signal(early_ready, (row, peer))
            return carry

        lax.fori_loop(middle, col_count, tell_late, 0)
        lax.fori_loop(0, middle - 1, tell_early, 0)

    @pl.when(late & (col != last_leader))
    def _():
        pl.semaphore_wait(barrier, 4)

    @pl.when(col == last_leader)
    def _():
        pl.semaphore_wait(barrier, 4 + col_count - middle - 1)

        def tell(peer, carry):
            signal(all_ready, (row, peer))
            return carry

        lax.fori_loop(middle, col_count - 1, tell, 0)

    @pl.when(late)
    def _():
        def tell(peer, carry):
            signal(late_ready.at[along - rounds // 2], (row, peer))
            return carry

        lax.fori_loop(0, middle, tell, 0)

    def up_slot(hop):
        return hop

    def down_slot(hop):
        return hop if hop == 0 or hop == reach else reach + hop

    def ring(way, part, hop):
        slot = up_slot if way == 0 else down_slot
        rows = pl.ds(part * depth, depth)
        source = stream_hbm.at[rows] if hop == 1 else gathered.at[0, slot(hop - 1), rows]
        return pltpu.make_async_remote_copy(
            src_ref=source,
            dst_ref=gathered.at[0, slot(hop), rows],
            send_sem=ring_send.at[way, part, hop - 1],
            recv_sem=ring_recv.at[way, part, hop - 1],
            device_id=(right if way == 0 else left, col),
            device_id_type=MESH,
        )

    def share(slot, part):
        rows = pl.ds(part * depth, depth)
        source = stream_hbm.at[rows] if slot == 0 else gathered.at[0, slot, rows]
        return pltpu.make_async_remote_copy(
            src_ref=source,
            dst_ref=gathered.at[1, slot, rows],
            send_sem=pair_send.at[slot, part],
            recv_sem=pair_recv.at[slot, part],
            device_id=(sibling, col),
            device_id_type=MESH,
        )

    def goes(way, part, hop):
        return hop <= (reach if way == part // (part_count // 2) else reach - 1)

    order = ((0, 0), (1, 2), (0, 1), (1, 3), (0, 2), (1, 0), (0, 3), (1, 1))
    def start_ring(turn):
        for way, part in order[2 * turn : 2 * turn + 2]:
            if goes(way, part, 1):
                ring(way, part, 1).start()
        share(0, turn).start()

    start_ring(0)

    def exchange(send_piece, wanted=None):
        for ahead, beside in offsets:
            peer = lax.rem(along + ahead, rounds) * width + lax.rem(across + beside, width)
            if wanted is None:
                send_piece(peer)
            else:
                pl.when(wanted(peer))(functools.partial(send_piece, peer))

    def is_early(peer):
        return peer < middle

    def is_late(peer):
        return peer >= middle

    def send_line(chunk, peer):
        pltpu.make_async_remote_copy(
            src_ref=lines_out.at[chunk, peer],
            dst_ref=lines_in.at[chunk, col],
            send_sem=lines_send,
            recv_sem=lines_recv.at[chunk],
            device_id=(row, peer),
            device_id_type=MESH,
        ).start()

    first_lines = functools.partial(send_line, 0)
    second_lines = functools.partial(send_line, 1)

    loads[0].wait()
    loads[1].wait()
    own = gathered.at[0, 0]
    chunk_size = per_peer // 2

    def make_lines(group):
        rows = pl.ds(group * walls, walls)
        speed = own[:, rows, :]
        flux = speed * normal[:, rows, :]
        both = jnp.concatenate(
            [speed.reshape(walls * walls, planes), flux.reshape(walls * walls, planes)], axis=1
        )
        moved = matmul(swap[...], both).astype(BF16)
        for kind in range(2):
            piece = moved[:, kind * planes : (kind + 1) * planes]
            chunk, rest = divmod(group * walls, length // 2)
            if chunk_size <= walls:
                peers = walls // chunk_size
                lines_out[chunk, pl.ds(rest // chunk_size, peers), kind] = piece.reshape(
                    peers, chunk_size, walls, planes
                )
            else:
                peer, start = divmod(rest, chunk_size)
                lines_out[chunk, peer, kind, pl.ds(start, walls)] = piece.reshape(
                    walls, walls, planes
                )

    groups = length // walls
    for group in range(groups // 2):
        make_lines(group)

    def keep_line(chunk):
        pltpu.make_async_copy(
            lines_out.at[chunk, col], lines_in.at[chunk, col], lines_recv.at[chunk]
        ).start()

    keep_line(0)
    start_ring(1)
    pl.when(late)(lambda: exchange(first_lines, is_early))
    start_ring(2)
    for group in range(groups // 2, groups):
        make_lines(group)
    keep_line(1)
    start_ring(3)

    @pl.when(late)
    def _():
        pl.when(col != last_leader)(lambda: pl.semaphore_wait(all_ready, 1))
        exchange(first_lines, is_late)

    loads[2].wait()
    loads[7].wait()
    plane_in = lax.broadcasted_iota(jnp.int32, (planes, planes), 0)
    plane_out = lax.broadcasted_iota(jnp.int32, (planes, planes), 1)
    distance = lax.rem(plane_in - plane_out + planes, planes)
    radius = coef_ref.shape[1] // 2
    banded = []
    for kind, weight in ((1, VISCOSITY), (0, -1.0)):
        band = jnp.zeros((planes, planes), F32)
        for offset in range(-radius, radius + 1):
            value = weight * coef_ref[kind, offset + radius]
            band = jnp.where(distance == offset % planes, value, band)
        banded.append(band)
    band = jnp.concatenate(banded, axis=0)
    coarse = band.astype(BF16)
    fine = (band - coarse.astype(F32)).astype(BF16)
    band = jnp.concatenate([coarse, fine], axis=1)

    for wall in range(walls):
        speed = own[wall]
        both = jnp.concatenate([speed, speed * span[wall]], axis=1)
        result = matmul(both, band)
        total[wall] = result[:, :planes] + result[:, planes:]

    first_quarter = col < middle // 2
    second_quarter = early & (col >= middle // 2)

    @pl.when(early)
    def _():
        pl.when(col != first_leader)(lambda: pl.semaphore_wait(early_ready, 1))
        exchange(first_lines, is_early)

    def lines_to_late():
        for plane in range(rounds // 2):
            pl.semaphore_wait(late_ready.at[plane], width)
            for beside in range(width):
                first_lines(middle + plane * width + lax.rem(across + beside, width))

    pl.when(second_quarter)(lines_to_late)

    loads[3].wait()
    loads[4].wait()
    for block in range(row_count):
        columns = pl.ds(block * length, length)
        line_matrix[block, :, pl.ds(0, length)] = second[:, columns] * BF16(VISCOSITY)
        line_matrix[block, :, pl.ds(length, length)] = -first[:, columns]

    def accumulate(where, slot, part):
        if slot <= reach:
            owner = lax.rem(chip - slot + chips, chips)
        else:
            owner = lax.rem(chip + slot - reach, chips)
        owner = owner * 2 + (core if where == 0 else 1 - core)
        matrix = line_matrix[owner]
        block = gathered.at[where, slot]
        for pair in range(depth // 2):
            wall = part * depth + 2 * pair
            speed = jnp.concatenate([block[wall], block[wall + 1]], axis=1)
            result = matmul(matrix, jnp.concatenate([speed, speed * speed], axis=0))
            total[wall] += result[:, :planes]
            total[wall + 1] += result[:, planes:]

    def shared(slot, part):
        share(slot, part).wait_recv()
        accumulate(1, slot, part)

    for part in range(part_count):
        accumulate(0, 0, part)

    for load in loads[5:7] + loads[8:10]:
        load.wait()
    height = wall_first.shape[0]
    chunk = min(128, height)
    diagonal = lax.broadcasted_iota(jnp.int32, (chunk, chunk), 0) == lax.broadcasted_iota(
        jnp.int32, (chunk, chunk), 1
    )
    for start in range(0, height, chunk):
        rows = pl.ds(start, chunk)
        one = jnp.sum(jnp.where(diagonal, metric1_ref[:, rows], 0.0), axis=1, keepdims=True)
        two = jnp.sum(jnp.where(diagonal, metric2_ref[:, rows], 0.0), axis=1, keepdims=True)
        first_rows = wall_first[rows, :].astype(F32)
        second_rows = wall_second[rows, :].astype(F32)
        viscous = VISCOSITY * (one * one * second_rows + two * first_rows)
        wall_matrix[rows, pl.ds(0, height)] = viscous.astype(BF16)
        wall_matrix[rows, pl.ds(height, height)] = (-(one * first_rows)).astype(BF16)

    def wall_terms(chunk):
        pltpu.make_async_copy(lines_out.at[chunk], lines_in.at[chunk], lines_recv.at[chunk]).wait()
        for position in range(0, chunk_size, 2):
            kinds = []
            for kind in range(2):
                both = [
                    lines_in[chunk, :, kind, position + i].reshape(height, planes)
                    for i in range(2)
                ]
                kinds.append(jnp.concatenate(both, axis=1))
            operand = jnp.concatenate(kinds, axis=0)
            result = matmul(wall_matrix[...], operand).astype(BF16)
            for i in range(2):
                terms_out[chunk, :, position + i] = result[
                    :, i * planes : (i + 1) * planes
                ].reshape(col_count, walls, planes)

        place = terms_in.at[chunk, pl.ds(col * chunk_size, chunk_size)]

        def send_term(peer):
            pltpu.make_async_remote_copy(
                src_ref=terms_out.at[chunk, peer],
                dst_ref=place,
                send_sem=terms_send,
                recv_sem=terms_recv.at[chunk],
                device_id=(row, peer),
                device_id_type=MESH,
            ).start()

        exchange(send_term)
        pltpu.make_async_copy(terms_out.at[chunk, col], place, terms_recv.at[chunk]).start()

    def add_terms(chunk):
        pltpu.make_async_copy(terms_in.at[chunk], terms_in.at[chunk], terms_recv.at[chunk]).wait()
        for group in range(0, groups // 2, 2):
            both = [
                terms_in[chunk, pl.ds((group + i) * walls, walls)].reshape(walls * walls, planes)
                for i in range(2)
            ]
            moved = matmul(swap[...], jnp.concatenate(both, axis=1))
            for i in range(2):
                rows = pl.ds(chunk * (length // 2) + (group + i) * walls, walls)
                term = moved[:, i * planes : (i + 1) * planes].reshape(walls, walls, planes)
                total[:, rows, :] += term

    send_second = functools.partial(exchange, second_lines)
    wall_first_half = functools.partial(wall_terms, 0)
    wall_second_half = functools.partial(wall_terms, 1)
    add_first_half = functools.partial(add_terms, 0)
    add_second_half = functools.partial(add_terms, 1)
    slots = {
        (1, 0): [
            (first_quarter, lines_to_late),
            (second_quarter, send_second),
            (late, send_second),
        ],
        (1, 1): [
            (first_quarter, send_second),
        ],
        (2, 0): [
            (second_quarter, wall_first_half),
            (late, wall_first_half),
        ],
        (2, 1): [
            (first_quarter, wall_first_half),
            (late, wall_second_half),
        ],
        (3, 0): [
            (second_quarter, wall_second_half),
        ],
        (3, 1): [
            (first_quarter, wall_second_half),
        ],
        (4, 0): [
            (None, add_first_half),
            (late, add_second_half),
        ],
    }

    pending = [(0, part) for part in range(part_count)]
    for hop in range(1, reach + 1):
        for half in range(2):
            arrived = []
            for way, part in order[half * part_count : (half + 1) * part_count]:
                if not goes(way, part, hop):
                    continue
                ring(way, part, hop).wait_recv()
                if goes(way, part, hop + 1):
                    ring(way, part, hop + 1).start()
                slot = (up_slot if way == 0 else down_slot)(hop)
                share(slot, part).start()
                arrived.append((slot, part))
            for slot, part in arrived:
                accumulate(0, slot, part)
            for slot, part in pending:
                shared(slot, part)
            pending = arrived
            for (at_hop, at_half), actions in slots.items():
                if (min(at_hop, reach), at_half) == (hop, half):
                    for condition, action in actions:
                        if condition is None:
                            action()
                        else:
                            pl.when(condition)(action)
    for slot, part in pending:
        shared(slot, part)

    loads[10].wait()
    position = lax.broadcasted_iota(jnp.int32, (1, planes), 1)
    limit = jnp.zeros((1, planes), jnp.int32)
    for block in range(counts_ref.shape[0]):
        limit = jnp.where(position // ZB == block, counts_ref[block], limit)
    mask = jnp.where(position % ZB < limit, 1.0, 0.0).astype(F32)

    pl.when(early)(add_second_half)
    for start in range(0, walls, depth):
        rows = pl.ds(start, depth)
        out_ref[rows] = (mask * total[rows]).astype(BF16)

    for hop in range(1, reach + 1):
        for way, part in order:
            if goes(way, part, hop):
                ring(way, part, hop).wait_send()
    for slot in range(chips):
        for part in range(part_count):
            share(slot, part).wait_send()
    others = pl.ds(0, col_count - 1)
    pltpu.make_async_copy(lines_out.at[:, others], lines_in.at[:, others], lines_send).wait()
    pltpu.make_async_copy(terms_out.at[:, others], terms_out.at[:, others], terms_send).wait()


def on_device(
    row_count,
    col_count,
    stream_speed,
    normal_speed,
    span_speed,
    stream_first,
    stream_second,
    wall_first,
    wall_second,
    metric1,
    metric2,
    span_coef,
    counts,
):
    shape = stream_speed.shape
    walls, length, planes = shape
    height = wall_first.shape[0]
    chips = row_count // 2
    reach = chips // 2
    per_peer = length // col_count
    hbm = pl.BlockSpec(memory_space=pltpu.HBM)
    exchange = (2, col_count, 2, per_peer // 2, walls, planes)
    dma = pltpu.SemaphoreType.DMA
    return pl.pallas_call(
        functools.partial(kernel, row_count, col_count),
        out_shape=jax.ShapeDtypeStruct(shape, BF16),
        in_specs=[hbm] * 11,
        out_specs=pl.BlockSpec(memory_space=pltpu.VMEM),
        scratch_shapes=[
            pltpu.VMEM((2, chips, *shape), BF16),
            pltpu.VMEM(shape, BF16),
            pltpu.VMEM(shape, BF16),
            pltpu.VMEM(stream_first.shape, BF16),
            pltpu.VMEM(stream_second.shape, BF16),
            pltpu.VMEM(wall_first.shape, BF16),
            pltpu.VMEM(wall_second.shape, BF16),
            pltpu.VMEM((row_count, length, 2 * length), BF16),
            pltpu.VMEM((height, 2 * height), BF16),
            pltpu.VMEM(exchange, BF16),
            pltpu.VMEM(exchange, BF16),
            pltpu.VMEM((2, col_count, per_peer // 2, walls, planes), BF16),
            pltpu.VMEM((2, length // 2, walls, planes), BF16),
            pltpu.VMEM(shape, F32),
            pltpu.VMEM((walls * walls, walls * walls), BF16),
            pltpu.VMEM((1, height), F32),
            pltpu.VMEM((1, height), F32),
            pltpu.SMEM(span_coef.shape, F32),
            pltpu.SMEM(counts.shape, jnp.int32),
            dma((11,)),
            dma((2, 4, reach)),
            dma((2, 4, reach)),
            dma((chips, 4)),
            dma((chips, 4)),
            dma,
            dma((2,)),
            dma,
            dma((2,)),
            pltpu.SemaphoreType.REGULAR,
            pltpu.SemaphoreType.REGULAR,
            pltpu.SemaphoreType.REGULAR((max(col_count // TORUS_WIDTH, 2) // 2,)),
        ],
        compiler_params=pltpu.CompilerParams(
            collective_id=0, has_side_effects=True, vmem_limit_bytes=53 * 2**20
        ),
    )(
        stream_speed,
        normal_speed,
        span_speed,
        stream_first,
        stream_second,
        wall_first,
        wall_second,
        metric1.reshape(1, -1),
        metric2.reshape(1, -1),
        span_coef,
        counts,
    )


def solution(mesh):
    placed = (
        P("col", "row", None),
        P("col", "row", None),
        P("col", "row", None),
        P("row", None),
        P("row", None),
        P(),
        P(),
        P(),
        P(),
        P(),
        P(),
    )
    return jax.shard_map(
        functools.partial(on_device, mesh.shape["row"], mesh.shape["col"]),
        mesh=mesh,
        in_specs=placed,
        out_specs=P("col", "row", None),
        check_vma=False,
    )
```

```python
import functools

import jax
import jax.numpy as jnp
from jax import lax
from jax.experimental import pallas as pl
from jax.experimental.pallas import tpu as pltpu
from jax.sharding import PartitionSpec as P

ZB = 4
TORUS_WIDTH = 4
VISCOSITY = 0.25
MESH = pl.DeviceIdType.MESH
F32 = jnp.float32
BF16 = jnp.bfloat16


def matmul(left, right):
    return jnp.dot(left, right, preferred_element_type=F32)


def swap_matrix(size):
    total = size * size
    row = lax.broadcasted_iota(jnp.int32, (total, total), 0)
    column = lax.broadcasted_iota(jnp.int32, (total, total), 1)
    same = (row // size == column % size) & (row % size == column // size)
    return jnp.where(same, 1.0, 0.0).astype(BF16)


def kernel(
    row_count,
    col_count,
    stream_hbm,
    normal_hbm,
    span_hbm,
    first_hbm,
    second_hbm,
    wall_first_hbm,
    wall_second_hbm,
    metric1_hbm,
    metric2_hbm,
    coef_hbm,
    counts_hbm,
    out_ref,
    gathered,
    normal,
    span,
    first,
    second,
    wall_first,
    wall_second,
    line_matrix,
    wall_matrix,
    lines_out,
    lines_in,
    terms_out,
    terms_in,
    total,
    swap,
    metric1_ref,
    metric2_ref,
    coef_ref,
    counts_ref,
    load_sem,
    ring_send,
    ring_recv,
    pair_send,
    pair_recv,
    lines_send,
    lines_recv,
    terms_send,
    terms_recv,
    early_ready,
    all_ready,
    late_ready,
):
    chips = row_count // 2
    reach = chips // 2
    walls, length, planes = normal.shape
    part_count = 4
    depth = walls // part_count
    per_peer = length // col_count
    row = lax.axis_index("row")
    col = lax.axis_index("col")
    chip, core = row // 2, lax.rem(row, 2)
    right = lax.rem(row + 2, row_count)
    left = lax.rem(row + row_count - 2, row_count)
    sibling = row + 1 - 2 * core

    pairs = (
        (stream_hbm, gathered.at[0, 0]),
        (normal_hbm, normal),
        (span_hbm, span),
        (second_hbm, second),
        (first_hbm, first),
        (wall_second_hbm, wall_second),
        (wall_first_hbm, wall_first),
        (coef_hbm, coef_ref),
        (metric1_hbm, metric1_ref),
        (metric2_hbm, metric2_ref),
        (counts_hbm, counts_ref),
    )
    loads = [pltpu.make_async_copy(a, b, load_sem.at[i]) for i, (a, b) in enumerate(pairs)]
    for load in loads:
        load.start()

    middle = col_count // 2
    first_leader, last_leader = middle - 1, col_count - 1
    early, late = col < middle, col >= middle
    width = min(TORUS_WIDTH, middle)
    rounds = col_count // width
    across, along = lax.rem(col, width), col // width
    far = [0] + [w for d in range(1, rounds // 2 + 1) for w in dict.fromkeys((d, rounds - d))]
    offsets = [(ahead, beside) for beside in range(width) for ahead in far if ahead or beside]
    barrier = pltpu.get_barrier_semaphore()

    def signal(semaphore, place):
        pl.semaphore_signal(semaphore, inc=1, device_id=place, device_id_type=MESH)

    for neighbour in (right, left, sibling):
        signal(barrier, (neighbour, col))
    pl.when(early & (col != first_leader))(lambda: signal(barrier, (row, first_leader)))
    pl.when(late & (col != last_leader))(lambda: signal(barrier, (row, last_leader)))

    swap[...] = swap_matrix(walls)

    @pl.when(early & (col != first_leader))
    def _():
        pl.semaphore_wait(barrier, 3)

    @pl.when(col == first_leader)
    def _():
        pl.semaphore_wait(barrier, 3 + middle - 1)

        def tell_late(peer, carry):
            signal(barrier, (row, peer))
            return carry

        def tell_early(peer, carry):
            signal(early_ready, (row, peer))
            return carry

        lax.fori_loop(middle, col_count, tell_late, 0)
        lax.fori_loop(0, middle - 1, tell_early, 0)

    @pl.when(late & (col != last_leader))
    def _():
        pl.semaphore_wait(barrier, 4)

    @pl.when(col == last_leader)
    def _():
        pl.semaphore_wait(barrier, 4 + col_count - middle - 1)

        def tell(peer, carry):
            signal(all_ready, (row, peer))
            return carry

        lax.fori_loop(middle, col_count - 1, tell, 0)

    @pl.when(late)
    def _():
        def tell(peer, carry):
            signal(late_ready.at[along - rounds // 2], (row, peer))
            return carry

        lax.fori_loop(0, middle, tell, 0)

    def up_slot(hop):
        return hop

    def down_slot(hop):
        return hop if hop == 0 or hop == reach else reach + hop

    def ring(way, part, hop):
        slot = up_slot if way == 0 else down_slot
        rows = pl.ds(part * depth, depth)
        source = stream_hbm.at[rows] if hop == 1 else gathered.at[0, slot(hop - 1), rows]
        return pltpu.make_async_remote_copy(
            src_ref=source,
            dst_ref=gathered.at[0, slot(hop), rows],
            send_sem=ring_send.at[way, part, hop - 1],
            recv_sem=ring_recv.at[way, part, hop - 1],
            device_id=(right if way == 0 else left, col),
            device_id_type=MESH,
        )

    def share(slot, part):
        rows = pl.ds(part * depth, depth)
        source = stream_hbm.at[rows] if slot == 0 else gathered.at[0, slot, rows]
        return pltpu.make_async_remote_copy(
            src_ref=source,
            dst_ref=gathered.at[1, slot, rows],
            send_sem=pair_send.at[slot, part],
            recv_sem=pair_recv.at[slot, part],
            device_id=(sibling, col),
            device_id_type=MESH,
        )

    def goes(way, part, hop):
        return hop <= (reach if way == part // (part_count // 2) else reach - 1)

    order = ((0, 0), (1, 2), (0, 1), (1, 3), (0, 2), (1, 0), (0, 3), (1, 1))
    def start_ring(turn):
        for way, part in order[2 * turn : 2 * turn + 2]:
            if goes(way, part, 1):
                ring(way, part, 1).start()
        share(0, turn).start()

    start_ring(0)

    def exchange(send_piece, wanted=None):
        for ahead, beside in offsets:
            peer = lax.rem(along + ahead, rounds) * width + lax.rem(across + beside, width)
            if wanted is None:
                send_piece(peer)
            else:
                pl.when(wanted(peer))(functools.partial(send_piece, peer))

    def is_early(peer):
        return peer < middle

    def is_late(peer):
        return peer >= middle

    def send_line(chunk, peer):
        pltpu.make_async_remote_copy(
            src_ref=lines_out.at[chunk, peer],
            dst_ref=lines_in.at[chunk, col],
            send_sem=lines_send,
            recv_sem=lines_recv.at[chunk],
            device_id=(row, peer),
            device_id_type=MESH,
        ).start()

    first_lines = functools.partial(send_line, 0)
    second_lines = functools.partial(send_line, 1)

    loads[0].wait()
    loads[1].wait()
    own = gathered.at[0, 0]
    chunk_size = per_peer // 2

    def make_lines(group):
        rows = pl.ds(group * walls, walls)
        speed = own[:, rows, :]
        flux = speed * normal[:, rows, :]
        both = jnp.concatenate(
            [speed.reshape(walls * walls, planes), flux.reshape(walls * walls, planes)], axis=1
        )
        moved = matmul(swap[...], both).astype(BF16)
        for kind in range(2):
            piece = moved[:, kind * planes : (kind + 1) * planes]
            chunk, rest = divmod(group * walls, length // 2)
            if chunk_size <= walls:
                peers = walls // chunk_size
                lines_out[chunk, pl.ds(rest // chunk_size, peers), kind] = piece.reshape(
                    peers, chunk_size, walls, planes
                )
            else:
                peer, start = divmod(rest, chunk_size)
                lines_out[chunk, peer, kind, pl.ds(start, walls)] = piece.reshape(
                    walls, walls, planes
                )

    groups = length // walls
    for group in range(groups // 2):
        make_lines(group)

    def keep_line(chunk):
        pltpu.make_async_copy(
            lines_out.at[chunk, col], lines_in.at[chunk, col], lines_recv.at[chunk]
        ).start()

    keep_line(0)
    start_ring(1)
    pl.when(late)(lambda: exchange(first_lines, is_early))
    start_ring(2)
    for group in range(groups // 2, groups):
        make_lines(group)
    keep_line(1)
    start_ring(3)

    @pl.when(late)
    def _():
        pl.when(col != last_leader)(lambda: pl.semaphore_wait(all_ready, 1))
        exchange(first_lines, is_late)

    loads[2].wait()
    loads[7].wait()
    plane_in = lax.broadcasted_iota(jnp.int32, (planes, planes), 0)
    plane_out = lax.broadcasted_iota(jnp.int32, (planes, planes), 1)
    distance = lax.rem(plane_in - plane_out + planes, planes)
    radius = coef_ref.shape[1] // 2
    banded = []
    for kind, weight in ((1, VISCOSITY), (0, -1.0)):
        band = jnp.zeros((planes, planes), F32)
        for offset in range(-radius, radius + 1):
            value = weight * coef_ref[kind, offset + radius]
            band = jnp.where(distance == offset % planes, value, band)
        banded.append(band)
    band = jnp.concatenate(banded, axis=0)
    coarse = band.astype(BF16)
    fine = (band - coarse.astype(F32)).astype(BF16)
    band = jnp.concatenate([coarse, fine], axis=1)

    for wall in range(walls):
        speed = own[wall]
        both = jnp.concatenate([speed, speed * span[wall]], axis=1)
        result = matmul(both, band)
        total[wall] = result[:, :planes] + result[:, planes:]

    first_quarter = col < middle // 2
    second_quarter = early & (col >= middle // 2)

    @pl.when(early)
    def _():
        pl.when(col != first_leader)(lambda: pl.semaphore_wait(early_ready, 1))
        exchange(first_lines, is_early)

    def lines_to_late():
        for plane in range(rounds // 2):
            pl.semaphore_wait(late_ready.at[plane], width)
            for beside in range(width):
                first_lines(middle + plane * width + lax.rem(across + beside, width))

    pl.when(second_quarter)(lines_to_late)

    loads[3].wait()
    loads[4].wait()
    for block in range(row_count):
        columns = pl.ds(block * length, length)
        line_matrix[block, :, pl.ds(0, length)] = second[:, columns] * BF16(VISCOSITY)
        line_matrix[block, :, pl.ds(length, length)] = -first[:, columns]

    def accumulate(where, slot, part):
        if slot <= reach:
            owner = lax.rem(chip - slot + chips, chips)
        else:
            owner = lax.rem(chip + slot - reach, chips)
        owner = owner * 2 + (core if where == 0 else 1 - core)
        matrix = line_matrix[owner]
        block = gathered.at[where, slot]
        for pair in range(depth // 2):
            wall = part * depth + 2 * pair
            speed = jnp.concatenate([block[wall], block[wall + 1]], axis=1)
            result = matmul(matrix, jnp.concatenate([speed, speed * speed], axis=0))
            total[wall] += result[:, :planes]
            total[wall + 1] += result[:, planes:]

    def shared(slot, part):
        share(slot, part).wait_recv()
        accumulate(1, slot, part)

    for part in range(part_count):
        accumulate(0, 0, part)

    for load in loads[5:7] + loads[8:10]:
        load.wait()
    height = wall_first.shape[0]
    chunk = min(128, height)
    diagonal = lax.broadcasted_iota(jnp.int32, (chunk, chunk), 0) == lax.broadcasted_iota(
        jnp.int32, (chunk, chunk), 1
    )
    for start in range(0, height, chunk):
        rows = pl.ds(start, chunk)
        one = jnp.sum(jnp.where(diagonal, metric1_ref[:, rows], 0.0), axis=1, keepdims=True)
        two = jnp.sum(jnp.where(diagonal, metric2_ref[:, rows], 0.0), axis=1, keepdims=True)
        first_rows = wall_first[rows, :].astype(F32)
        second_rows = wall_second[rows, :].astype(F32)
        viscous = VISCOSITY * (one * one * second_rows + two * first_rows)
        wall_matrix[rows, pl.ds(0, height)] = viscous.astype(BF16)
        wall_matrix[rows, pl.ds(height, height)] = (-(one * first_rows)).astype(BF16)

    def place_of(chunk):
        return terms_in.at[chunk, pl.ds(col * chunk_size, chunk_size)]

    def send_term(chunk, peer):
        pltpu.make_async_remote_copy(
            src_ref=terms_out.at[chunk, peer],
            dst_ref=place_of(chunk),
            send_sem=terms_send,
            recv_sem=terms_recv.at[chunk],
            device_id=(row, peer),
            device_id_type=MESH,
        ).start()

    first_terms = functools.partial(send_term, 0)
    second_terms = functools.partial(send_term, 1)

    def wall_terms(chunk):
        pltpu.make_async_copy(lines_out.at[chunk], lines_in.at[chunk], lines_recv.at[chunk]).wait()
        for position in range(0, chunk_size, 2):
            kinds = []
            for kind in range(2):
                both = [
                    lines_in[chunk, :, kind, position + i].reshape(height, planes)
                    for i in range(2)
                ]
                kinds.append(jnp.concatenate(both, axis=1))
            operand = jnp.concatenate(kinds, axis=0)
            result = matmul(wall_matrix[...], operand).astype(BF16)
            for i in range(2):
                terms_out[chunk, :, position + i] = result[
                    :, i * planes : (i + 1) * planes
                ].reshape(col_count, walls, planes)

        if chunk == 0:
            pl.when(late)(lambda: exchange(first_terms))
            pl.when(early)(lambda: exchange(first_terms, is_early))
        else:
            exchange(second_terms)
            pl.when(early)(lambda: exchange(first_terms, is_late))
        pltpu.make_async_copy(
            terms_out.at[chunk, col], place_of(chunk), terms_recv.at[chunk]
        ).start()

    def add_terms(chunk):
        pltpu.make_async_copy(terms_in.at[chunk], terms_in.at[chunk], terms_recv.at[chunk]).wait()
        for group in range(0, groups // 2, 2):
            both = [
                terms_in[chunk, pl.ds((group + i) * walls, walls)].reshape(walls * walls, planes)
                for i in range(2)
            ]
            moved = matmul(swap[...], jnp.concatenate(both, axis=1))
            for i in range(2):
                rows = pl.ds(chunk * (length // 2) + (group + i) * walls, walls)
                term = moved[:, i * planes : (i + 1) * planes].reshape(walls, walls, planes)
                total[:, rows, :] += term

    send_second = functools.partial(exchange, second_lines)
    wall_first_half = functools.partial(wall_terms, 0)
    wall_second_half = functools.partial(wall_terms, 1)
    add_first_half = functools.partial(add_terms, 0)
    add_second_half = functools.partial(add_terms, 1)
    slots = {
        (1, 0): [
            (first_quarter, lines_to_late),
            (second_quarter, send_second),
            (late, send_second),
        ],
        (1, 1): [
            (first_quarter, send_second),
        ],
        (2, 0): [
            (second_quarter, wall_first_half),
            (late, wall_first_half),
        ],
        (2, 1): [
            (first_quarter, wall_first_half),
            (late, wall_second_half),
        ],
        (3, 0): [
            (second_quarter, wall_second_half),
        ],
        (3, 1): [
            (first_quarter, wall_second_half),
        ],
        (4, 0): [
            (None, add_first_half),
            (late, add_second_half),
        ],
    }

    pending = [(0, part) for part in range(part_count)]
    for hop in range(1, reach + 1):
        for half in range(2):
            arrived = []
            for way, part in order[half * part_count : (half + 1) * part_count]:
                if not goes(way, part, hop):
                    continue
                ring(way, part, hop).wait_recv()
                if goes(way, part, hop + 1):
                    ring(way, part, hop + 1).start()
                slot = (up_slot if way == 0 else down_slot)(hop)
                share(slot, part).start()
                arrived.append((slot, part))
            for slot, part in arrived:
                accumulate(0, slot, part)
            for slot, part in pending:
                shared(slot, part)
            pending = arrived
            for (at_hop, at_half), actions in slots.items():
                if (min(at_hop, reach), at_half) == (hop, half):
                    for condition, action in actions:
                        if condition is None:
                            action()
                        else:
                            pl.when(condition)(action)
    for slot, part in pending:
        shared(slot, part)

    loads[10].wait()
    position = lax.broadcasted_iota(jnp.int32, (1, planes), 1)
    limit = jnp.zeros((1, planes), jnp.int32)
    for block in range(counts_ref.shape[0]):
        limit = jnp.where(position // ZB == block, counts_ref[block], limit)
    mask = jnp.where(position % ZB < limit, 1.0, 0.0).astype(F32)

    pl.when(early)(add_second_half)
    for start in range(0, walls, depth):
        rows = pl.ds(start, depth)
        out_ref[rows] = (mask * total[rows]).astype(BF16)

    for hop in range(1, reach + 1):
        for way, part in order:
            if goes(way, part, hop):
                ring(way, part, hop).wait_send()
    for slot in range(chips):
        for part in range(part_count):
            share(slot, part).wait_send()
    others = pl.ds(0, col_count - 1)
    pltpu.make_async_copy(lines_out.at[:, others], lines_in.at[:, others], lines_send).wait()
    pltpu.make_async_copy(terms_out.at[:, others], terms_out.at[:, others], terms_send).wait()


def on_device(
    row_count,
    col_count,
    stream_speed,
    normal_speed,
    span_speed,
    stream_first,
    stream_second,
    wall_first,
    wall_second,
    metric1,
    metric2,
    span_coef,
    counts,
):
    shape = stream_speed.shape
    walls, length, planes = shape
    height = wall_first.shape[0]
    chips = row_count // 2
    reach = chips // 2
    per_peer = length // col_count
    hbm = pl.BlockSpec(memory_space=pltpu.HBM)
    exchange = (2, col_count, 2, per_peer // 2, walls, planes)
    dma = pltpu.SemaphoreType.DMA
    return pl.pallas_call(
        functools.partial(kernel, row_count, col_count),
        out_shape=jax.ShapeDtypeStruct(shape, BF16),
        in_specs=[hbm] * 11,
        out_specs=pl.BlockSpec(memory_space=pltpu.VMEM),
        scratch_shapes=[
            pltpu.VMEM((2, chips, *shape), BF16),
            pltpu.VMEM(shape, BF16),
            pltpu.VMEM(shape, BF16),
            pltpu.VMEM(stream_first.shape, BF16),
            pltpu.VMEM(stream_second.shape, BF16),
            pltpu.VMEM(wall_first.shape, BF16),
            pltpu.VMEM(wall_second.shape, BF16),
            pltpu.VMEM((row_count, length, 2 * length), BF16),
            pltpu.VMEM((height, 2 * height), BF16),
            pltpu.VMEM(exchange, BF16),
            pltpu.VMEM(exchange, BF16),
            pltpu.VMEM((2, col_count, per_peer // 2, walls, planes), BF16),
            pltpu.VMEM((2, length // 2, walls, planes), BF16),
            pltpu.VMEM(shape, F32),
            pltpu.VMEM((walls * walls, walls * walls), BF16),
            pltpu.VMEM((1, height), F32),
            pltpu.VMEM((1, height), F32),
            pltpu.SMEM(span_coef.shape, F32),
            pltpu.SMEM(counts.shape, jnp.int32),
            dma((11,)),
            dma((2, 4, reach)),
            dma((2, 4, reach)),
            dma((chips, 4)),
            dma((chips, 4)),
            dma,
            dma((2,)),
            dma,
            dma((2,)),
            pltpu.SemaphoreType.REGULAR,
            pltpu.SemaphoreType.REGULAR,
            pltpu.SemaphoreType.REGULAR((max(col_count // TORUS_WIDTH, 2) // 2,)),
        ],
        compiler_params=pltpu.CompilerParams(
            collective_id=0, has_side_effects=True, vmem_limit_bytes=53 * 2**20
        ),
    )(
        stream_speed,
        normal_speed,
        span_speed,
        stream_first,
        stream_second,
        wall_first,
        wall_second,
        metric1.reshape(1, -1),
        metric2.reshape(1, -1),
        span_coef,
        counts,
    )


def solution(mesh):
    placed = (
        P("col", "row", None),
        P("col", "row", None),
        P("col", "row", None),
        P("row", None),
        P("row", None),
        P(),
        P(),
        P(),
        P(),
        P(),
        P(),
    )
    return jax.shard_map(
        functools.partial(on_device, mesh.shape["row"], mesh.shape["col"]),
        mesh=mesh,
        in_specs=placed,
        out_specs=P("col", "row", None),
        check_vma=False,
    )
```
